32 devices in a mesh: rows: 8 (over z, y), cols: 4 (over x, core).
Axes of the slice: x: 2, y: 2, z: 4, core: 2. Of those that a mesh axis runs over, the one named last changes fastest.
Arguments:
- points: float32 [8192, 1024], P('rows', 'cols'), may hold values from -6 to 6
- pivots: int32 [2, 512], replicated, may hold values from 0 to 8191, as said below
- targets: float32 [8192, 256], P('rows', 'cols'), may hold values from -6 to 6
Outputs:
- factor: float32 [8192, 1024], P(('rows', 'cols'))
- projection: float32 [1024, 256], P(None, 'cols')
The draws below stay inside these ranges and needn't reach their ends.
Inputs may be any that keep to these rules, and one draw needn't show every extreme that they name: All 1024 indices of both blocks are distinct. The points of one index of rows (an aligned run of 1024 indices) hold at most 512 pivots of the two blocks together, and in every draw some index of rows holds exactly 512.
All inputs are finite; a program needn't handle non-finite values.
Results may differ from the reference program's by a relative error of at most 0.0003.
Values sent between devices are 32-bit elements; how exact they have to be, the bound alone decides.
No kernel may reach another device: no remote copies, remote signals or barrier semaphores. Data moves between devices by JAX's collectives and lax.ppermute only.
A program may use at most 64 MiB of HBM per device.

```python
import math
import jax
import jax.numpy as jnp
from jax import lax

E = 1024
BLOCK = 512
TGT = 256
ROWS_PER_SHARD = 1024
NPTS = 8192
MOST = 512


def draw_pivots(key, part):
    holding_device_numbers = NPTS // ROWS_PER_SHARD
    most = MOST
    keys = jax.random.split(jax.random.fold_in(key, 17), 5)
    threshold_amount = jax.random.randint(keys[0], (holding_device_numbers,), 0, 4)
    preferred_points = jax.random.randint(keys[1], (), 0, holding_device_numbers)
    random_jitter = jax.random.randint(keys[2], (holding_device_numbers, most), 0, 1024)
    extra_multiplier = jnp.where(jnp.arange(holding_device_numbers) == preferred_points, 4096, 0)
    selection_criterion = random_jitter + threshold_amount[:, None] * 256 + extra_multiplier[:, None]
    distinct = selection_criterion * (holding_device_numbers * most) + jnp.arange(holding_device_numbers * most).reshape(holding_device_numbers, most)
    _, chosen = lax.top_k(distinct.reshape(-1), 2 * BLOCK)
    slot_owner = chosen // most
    slot = chosen % most
    shuffled = jax.random.randint(keys[3], (holding_device_numbers, ROWS_PER_SHARD), 0, 2 ** 18) * ROWS_PER_SHARD + jnp.arange(ROWS_PER_SHARD)[None, :]
    order = jnp.argsort(shuffled, axis=1, stable=True).astype(jnp.int32)
    inside = order[slot_owner, slot]
    position_list = slot_owner * ROWS_PER_SHARD + inside
    mixing = jax.random.permutation(keys[4], 2 * BLOCK)
    return position_list[mixing].reshape(2, BLOCK).astype(jnp.int32)


def shard_levels(rng, shape, shards, low, top_value):
    factor_of = 1.0
    for dim, parts in shards:
        draws = jax.random.uniform(jax.random.fold_in(jax.random.fold_in(rng, 6), dim), (parts,), jnp.float32, low / len(shards), top_value / len(shards))
        factor_of = factor_of * jnp.repeat(jnp.exp(draws), shape[dim] // parts).reshape((-1,) + (1,) * (len(shape) - 1 - dim))
    return factor_of


def bell_draw(rng, extent, scale, bound, shards=(), kind=jnp.bfloat16):
    values = jax.random.normal(rng, extent, jnp.float32) * scale
    if len(shards) > 0:
        values = shard_levels(rng, extent, shards, -0.22, 0.18) * values
    return jnp.clip(values, min=-bound, max=bound).astype(kind)


def setup_inputs(seed: int = 0) -> dict:
    key_list = jax.random.split(jax.random.key(seed), 4)
    points = bell_draw(key_list[0], (NPTS, E), 1.0, 6.0, ((0, 8), (1, 4)), jnp.float32)
    pivots = draw_pivots(jax.random.fold_in(key_list[3], 71), 0)
    targets = bell_draw(key_list[2], (NPTS, TGT), 1.0, 6.0, ((0, 8), (1, 4)), jnp.float32)
    return dict(points=points, pivots=pivots, targets=targets)


RIDGE = 0.001

def right_side_solve(low, values):
    return lax.linalg.triangular_solve(low, values, left_side=False, lower=True, transpose_a=True)

def reference(points, pivots, targets):
    highest = lax.Precision.HIGHEST
    block = pivots.shape[1]
    flat = pivots.reshape(-1)
    chosen = points[flat]
    norms = lax.optimization_barrier(jnp.sum(points * points, axis=1))
    chosen_norms = lax.optimization_barrier(jnp.sum(chosen * chosen, axis=1))
    cross = jnp.dot(points.astype(jnp.float32), chosen.T.astype(jnp.float32), precision=highest, preferred_element_type=jnp.float32)
    dist = norms[:, None] + chosen_norms[None, :] - 2.0 * cross
    kern = jnp.exp(-dist / (2.0 * E))
    first = kern[:, :block]
    second = kern[:, block:]
    identity = jnp.eye(block, dtype=jnp.float32)
    low_one = jnp.linalg.cholesky(first[pivots[0]] + RIDGE * identity)
    factor_one = right_side_solve(low_one, first)
    crossed = factor_one[pivots[1]]
    resid = second - jnp.dot(factor_one.astype(jnp.float32), crossed.T.astype(jnp.float32), precision=highest, preferred_element_type=jnp.float32)
    low_two = jnp.linalg.cholesky(resid[pivots[1]] + RIDGE * identity)
    second_lower_matrix = right_side_solve(low_two, resid)
    factor = jnp.concatenate([factor_one, second_lower_matrix], axis=1)
    projection = jnp.dot(factor.T.astype(jnp.float32), targets.astype(jnp.float32), precision=highest, preferred_element_type=jnp.float32) / math.sqrt(NPTS)
    return (factor, projection)
```

```python
import functools
import math

import jax
import jax.numpy as jnp
from jax import lax
from jax.experimental import pallas as pl
from jax.experimental.pallas import tpu as pltpu
from jax.sharding import PartitionSpec as P

HI = lax.Precision.HIGHEST
T = 8
RIDGE = 0.001


def diag_inverse(rows, width, sub):
    tiles = width // T
    per = sub // T
    lane = lax.broadcasted_iota(jnp.int32, (T, width), 1)
    sl = lax.broadcasted_iota(jnp.int32, (T, width), 0)
    rows = list(rows)
    scale = [None] * tiles
    for s0 in range(0, tiles, per):
        hi = s0 + per
        recs = []
        for t in range(s0, hi):
            c = {}
            for s in range(t, hi):
                for k in range(T):
                    c[s, k] = jnp.broadcast_to(rows[s][:, T * t + k : T * t + k + 1], (T, width))
            dv = jnp.ones((T, width), jnp.float32)
            for k in range(T):
                col = T * t + k
                d = jnp.broadcast_to(c[t, k][k : k + 1, :], (T, width))
                r = 1.0 / d
                dv = jnp.where(sl == k, d, dv)
                p = jnp.where(lane == col, 1.0, jnp.broadcast_to(rows[t][k : k + 1, :], (T, width)))
                heads = {q: jnp.broadcast_to(c[t, q][k : k + 1, :], (T, width)) for q in range(k + 1, T)}
                for s in range(t, hi):
                    ck = c[s, k]
                    if s == t:
                        ck = jnp.where(sl > k, ck, 0.0)
                    m = ck * r
                    for q in range(k + 1, T):
                        c[s, q] = c[s, q] - m * heads[q]
                    if s == t:
                        base = jnp.where(lane == col, jnp.where(sl > k, 0.0, jnp.where(sl == k, 1.0, rows[s])), rows[s])
                    else:
                        base = jnp.where(lane == col, 0.0, rows[s])
                    rows[s] = base - m * p
            scale[t] = lax.rsqrt(dv)
            recs.append(1.0 / dv)
        if hi < tiles:
            x = jnp.concatenate(
                [jnp.where((lane > sl + T * t) & (lane < T * hi), 0.0, rows[t]) for t in range(s0, hi)], axis=0
            )
            w = x * jnp.concatenate(recs, axis=0)
            wt = w[:, T * hi :].T
            upd = lax.dot_general(wt, x, (((1,), (0,)), ((), ())), precision=HI, preferred_element_type=jnp.float32)
            for s in range(hi, tiles):
                keep = jnp.where((lane >= T * s0) & (lane < T * hi), 0.0, rows[s])
                rows[s] = keep - upd[T * (s - hi) : T * (s - hi + 1), :]
    out = []
    for t in range(tiles):
        out.append(jnp.where(lane <= sl + T * t, rows[t] * scale[t], 0.0))
    return jnp.concatenate(out, axis=0)

def chol_kernel(width, sub, ridge, a_ref, o_ref, d_ref):
    n = a_ref.shape[0]
    o_ref[...] = a_ref[...]
    row = lax.broadcasted_iota(jnp.int32, (n, width), 0)
    def step(j, _):
        off = pl.multiple_of(j * width, width)
        eye = (lax.broadcasted_iota(jnp.int32, (width, width), 0) == lax.broadcasted_iota(jnp.int32, (width, width), 1)).astype(jnp.float32)
        d_ref[...] = o_ref[pl.ds(off, width), pl.ds(off, width)] + ridge * eye
        m = diag_inverse([d_ref[pl.ds(T * t, T), :] for t in range(width // T)], width, sub)
        col = o_ref[:, pl.ds(off, width)]
        low = lax.dot_general(col, m, (((1,), (1,)), ((), ())), precision=HI, preferred_element_type=jnp.float32)
        low = jnp.where(row >= off + width, low, 0.0)
        o_ref[pl.ds(off, width), pl.ds(off, width)] = eye
        x = jnp.dot(m, o_ref[pl.ds(off, width), :], precision=HI, preferred_element_type=jnp.float32)
        o_ref[:, pl.ds(off, width)] = jnp.where(row >= off + width, 0.0, o_ref[:, pl.ds(off, width)])
        o_ref[...] = o_ref[...] - jnp.dot(low, x, precision=HI, preferred_element_type=jnp.float32)
        o_ref[pl.ds(off, width), :] = x
        return 0
    lax.fori_loop(0, n // width, step, 0)
    rr = lax.broadcasted_iota(jnp.int32, (n, n), 0)
    cc = lax.broadcasted_iota(jnp.int32, (n, n), 1)
    o_ref[...] = jnp.where(cc <= rr, o_ref[...], 0.0)

def chol_inverse(a, width=128, sub=64, ridge=RIDGE):
    n = a.shape[0]
    return pl.pallas_call(
        functools.partial(chol_kernel, width, sub, ridge),
        out_shape=jax.ShapeDtypeStruct((n, n), jnp.float32),
        in_specs=[pl.BlockSpec(memory_space=pltpu.VMEM)],
        out_specs=pl.BlockSpec(memory_space=pltpu.VMEM),
        scratch_shapes=[pltpu.VMEM((width, width), jnp.float32)],
        cost_estimate=pl.CostEstimate(flops=n * n * n * 8, bytes_accessed=8 * n * n, transcendentals=0),
        compiler_params=pltpu.CompilerParams(vmem_limit_bytes=32 << 20),
        name="chol",
    )(a)


def place_kernel(idx_ref, me_ref, pts_ref, a_ref, b_ref):
    rows, width = pts_ref.shape
    pts = pts_ref[...]
    high = pts.astype(jnp.bfloat16)
    rest = pts - high.astype(jnp.float32)
    mid = rest.astype(jnp.bfloat16)
    tail = (rest - mid.astype(jnp.float32)).astype(jnp.bfloat16)
    base = me_ref[0] * rows
    for h, out in enumerate((a_ref, b_ref)):
        block = idx_ref.shape[1]
        idx = jnp.broadcast_to(idx_ref[h : h + 1, :] - base, (8, block)).T[:, :1]
        hot = (idx == lax.broadcasted_iota(jnp.int32, (block, rows), 1)).astype(jnp.float32).astype(jnp.bfloat16)
        total = jnp.dot(hot, tail, preferred_element_type=jnp.float32)
        total += jnp.dot(hot, mid, preferred_element_type=jnp.float32)
        out[...] = total + jnp.dot(hot, high, preferred_element_type=jnp.float32)


def place(pivots, me, points):
    block = pivots.shape[1]
    rows, width = points.shape
    shape = jax.ShapeDtypeStruct((block, width), jnp.float32)
    vmem = pl.BlockSpec(memory_space=pltpu.VMEM)
    return pl.pallas_call(
        place_kernel,
        out_shape=(shape, shape),
        in_specs=[vmem, pl.BlockSpec(memory_space=pltpu.SMEM), vmem],
        out_specs=(vmem, vmem),
        cost_estimate=pl.CostEstimate(flops=12 * block * rows * width, bytes_accessed=8 * rows * width, transcendentals=0),
        compiler_params=pltpu.CompilerParams(vmem_limit_bytes=32 << 20),
        name="place",
    )(pivots, me.reshape(1), points)


def swap(x, mask):
    size = lax.axis_size("cols")
    return lax.ppermute(x, "cols", [(i, i ^ mask) for i in range(size)])


def scatter_sum(x):
    n = lax.axis_size("rows")
    x = lax.all_to_all(x.reshape((n, x.shape[0] // n) + x.shape[1:]), "rows", 0, 0)
    return jnp.sum(x, axis=0)


def gather_rows(x):
    n = lax.axis_size("rows")
    y = lax.all_to_all(jnp.broadcast_to(x[None], (n,) + x.shape), "rows", 0, 0)
    return y.reshape((n * x.shape[0],) + x.shape[1:])


def spread(x):
    one = swap(x, 1)
    two = swap(x, 2)
    return [x, one, two, swap(two, 1)]


def exchange(x):
    size = lax.axis_size("cols")
    me = lax.axis_index("cols")
    n = x.shape[0] // size
    out = []
    for k in range(size):
        part = lax.dynamic_slice_in_dim(x, (me ^ k) * n, n, 0)
        out.append(part if k == 0 else swap(part, k))
    return out


def exchange_cols(x):
    size = lax.axis_size("cols")
    y = lax.all_to_all(x.reshape(size, x.shape[0] // size, x.shape[1]), "cols", 0, 0)
    return [y[i] for i in range(size)]


def gauss(left, right, precision):
    cross = lax.dot_general(left, right, (((1,), (1,)), ((), ())), precision=precision, preferred_element_type=jnp.float32)
    ln = jnp.sum(left * left, axis=1)
    rn = jnp.sum(right * right, axis=1)
    dist = ln[:, None] + rn[None, :] - 2.0 * cross
    return jnp.exp(-dist / (2.0 * left.shape[1]))


def mul_t(a, b):
    return lax.dot_general(a, b, (((1,), (1,)), ((), ())), precision=HI, preferred_element_type=jnp.float32)


def shards(points, pivots, targets):
    near = lax.Precision.HIGH
    rows_dev = points.shape[0]
    nrows = lax.axis_size("rows")
    ncols = lax.axis_size("cols")
    assert ncols == 4
    me = lax.axis_index("rows")
    place_a, place_b = place(pivots, me, points)
    part_a = scatter_sum(place_a)
    own = jnp.concatenate(exchange(points), axis=1)
    goal = jnp.concatenate(exchange_cols(targets), axis=1)
    part_b = scatter_sum(place_b)
    piv_a = jnp.concatenate(spread(gather_rows(part_a)), axis=1)
    piv_b = jnp.concatenate(spread(gather_rows(part_b)), axis=1)
    inv_one = chol_inverse(gauss(piv_a, piv_a, near))
    side = gauss(piv_b, piv_a, near)
    crossed = mul_t(side, inv_one)
    schur = gauss(piv_b, piv_b, near) - mul_t(crossed, crossed)
    inv_two = chol_inverse(schur)
    kern = [gauss(own, p, near) for p in (piv_a, piv_b)]
    heads = []
    for k in kern:
        g = lax.dot_general(goal, k, (((0,), (0,)), ((), ())), precision=HI, preferred_element_type=jnp.float32)
        heads.append(g)
    total = jnp.concatenate(heads, axis=1)
    total = sum(exchange(total))
    total = gather_rows(scatter_sum(total))
    block = pivots.shape[1]
    own_n = own.shape[0]
    first = jnp.concatenate([kern[0], total[:, :block]], axis=0)
    second = jnp.concatenate([kern[1], total[:, block:]], axis=0)
    fac_one = mul_t(first, inv_one)
    fac_two = mul_t(second - mul_t(fac_one, crossed), inv_two)
    both = jnp.concatenate([fac_one, fac_two], axis=1)
    factor = both[:own_n]
    projection = both[own_n:].T * (1.0 / math.sqrt(rows_dev * nrows))
    return (factor, projection)


def solution(mesh):
    return jax.shard_map(
        shards,
        mesh=mesh,
        in_specs=(P("rows", "cols"), P(), P("rows", "cols")),
        out_specs=(P(("rows", "cols"), None), P(None, "cols")),
        check_vma=False,
    )
```

```python
import functools
import math

import jax
import jax.numpy as jnp
from jax import lax
from jax.experimental import pallas as pl
from jax.experimental.pallas import tpu as pltpu
from jax.sharding import PartitionSpec as P

HI = lax.Precision.HIGHEST
NEAR = lax.Precision.HIGH
T = 8
RIDGE = 0.001


def split(x):
    h = x.astype(jnp.bfloat16)
    r = x - h.astype(jnp.float32)
    m = r.astype(jnp.bfloat16)
    return h, m, (r - m.astype(jnp.float32)).astype(jnp.bfloat16)


def left_stack(x):
    h, m, l = split(x)
    return jnp.concatenate([h, h, m, h, m, l], axis=1)


def right_stack(x, axis):
    h, m, l = split(x)
    return jnp.concatenate([h, m, h, l, m, h], axis=axis)


def stack_dot(a, b, axis):
    return lax.dot_general(
        left_stack(a), right_stack(b, axis), (((1,), (axis,)), ((), ())), preferred_element_type=jnp.float32
    )


def diag_inverse(rows, width, sub):
    tiles = width // T
    per = sub // T
    lane = lax.broadcasted_iota(jnp.int32, (T, width), 1)
    sl = lax.broadcasted_iota(jnp.int32, (T, width), 0)
    rows = list(rows)
    scale = [None] * tiles
    for s0 in range(0, tiles, per):
        hi = s0 + per
        recs = []
        for t in range(s0, hi):
            c = {}
            for s in range(t, hi):
                for k in range(T):
                    c[s, k] = jnp.broadcast_to(rows[s][:, T * t + k : T * t + k + 1], (T, width)) + 0.0
            dv = jnp.ones((T, width), jnp.float32)
            for k in range(0, T, 2):
                col = T * t + k
                def row_of(v, i):
                    return jnp.broadcast_to(v[i : i + 1, :], (T, width))
                a = row_of(c[t, k], k)
                b = row_of(c[t, k], k + 1)
                e = row_of(c[t, k + 1], k + 1)
                det = a * e - b * b
                ra = 1.0 / a
                rd = 1.0 / det
                rad = ra * rd
                dv = jnp.where(sl == k, a, jnp.where(sl == k + 1, det * ra, dv))
                r0 = row_of(rows[t], k)
                r1 = row_of(rows[t], k + 1)
                p0 = jnp.where(lane == col, 1.0, r0)
                p1 = jnp.where(lane == col, 0.0, jnp.where(lane == col + 1, 1.0, r1))
                pv = a * p1 - b * jnp.where(lane == col + 1, 0.0, p0)
                new1 = jnp.where(lane == col + 1, 1.0, pv * ra)
                heads = {q: row_of(c[t, q], k) for q in range(k + 2, T)}
                q0 = jnp.where(lane == col + 1, 0.0, p0) * ra
                q1 = pv * rad
                tails, scaled_heads, scaled_tails = {}, {}, {}
                for s in range(t, hi):
                    c0, c1 = c[s, k], c[s, k + 1]
                    if s == t:
                        c0 = jnp.where(sl > k + 1, c0, 0.0)
                        c1 = jnp.where(sl > k + 1, c1, 0.0)
                    w = a * c1 - b * c0
                    for q in range(k + 2, T):
                        if s == t:
                            tails[q] = row_of(w, q)
                            scaled_heads[q] = heads[q] * ra
                            scaled_tails[q] = tails[q] * rad
                            c[s, q] = c[s, q] - c0 * scaled_heads[q] - (w * tails[q]) * rad
                        else:
                            c[s, q] = c[s, q] - c0 * scaled_heads[q] - w * scaled_tails[q]
                    base = rows[s]
                    if s == t:
                        base = jnp.where(((lane == col) | (lane == col + 1)) & (sl > k + 1), 0.0, base)
                        base = jnp.where(sl == k, p0, jnp.where(sl == k + 1, new1, base))
                    else:
                        base = jnp.where((lane == col) | (lane == col + 1), 0.0, base)
                    rows[s] = base - c0 * q0 - w * q1
            scale[t] = lax.rsqrt(dv)
            recs.append(1.0 / dv)
        if hi < tiles:
            x = jnp.concatenate(
                [jnp.where((lane > sl + T * t) & (lane < T * hi), 0.0, rows[t]) for t in range(s0, hi)], axis=0
            )
            w = x * jnp.concatenate(recs, axis=0)
            upd = stack_dot(w[:, T * hi :].T, x, 0)
            for s in range(hi, tiles):
                keep = jnp.where((lane >= T * s0) & (lane < T * hi), 0.0, rows[s])
                rows[s] = keep - upd[T * (s - hi) : T * (s - hi + 1), :]
    out = []
    for t in range(tiles):
        out.append(jnp.where(lane <= sl + T * t, rows[t] * scale[t], 0.0))
    return jnp.concatenate(out, axis=0)

def chol_kernel(width, sub, first, last, a_ref, o_ref, d_ref):
    n = a_ref.shape[0]
    if first == 0:
        o_ref[...] = a_ref[...]
    row = lax.broadcasted_iota(jnp.int32, (n, width), 0)

    def step(j, _):
        off = pl.multiple_of(j * width, width)
        eye = (
            lax.broadcasted_iota(jnp.int32, (width, width), 0) == lax.broadcasted_iota(jnp.int32, (width, width), 1)
        ).astype(jnp.float32)
        d_ref[...] = o_ref[pl.ds(off, width), pl.ds(off, width)] + RIDGE * eye
        m = diag_inverse([d_ref[pl.ds(T * t, T), :] for t in range(width // T)], width, sub)
        col = o_ref[:, pl.ds(off, width)]
        low = jnp.where(row >= off + width, stack_dot(col, m, 1), 0.0)
        o_ref[pl.ds(off, width), pl.ds(off, width)] = eye
        x = stack_dot(m, o_ref[pl.ds(off, width), :], 0)
        o_ref[:, pl.ds(off, width)] = jnp.where(row >= off + width, 0.0, o_ref[:, pl.ds(off, width)])
        o_ref[...] = o_ref[...] - stack_dot(low, x, 0)
        o_ref[pl.ds(off, width), :] = x
        return 0

    lax.fori_loop(first, last, step, 0)
    if last * width == n:
        rr = lax.broadcasted_iota(jnp.int32, (n, n), 0)
        cc = lax.broadcasted_iota(jnp.int32, (n, n), 1)
        o_ref[...] = jnp.where(cc <= rr, o_ref[...], 0.0)


def chol_inverse(a, first=0, last=None, width=128, sub=64):
    n = a.shape[0]
    last = n // width if last is None else last
    return pl.pallas_call(
        functools.partial(chol_kernel, width, sub, first, last),
        out_shape=jax.ShapeDtypeStruct((n, n), jnp.float32),
        in_specs=[pl.BlockSpec(memory_space=pltpu.VMEM)],
        out_specs=pl.BlockSpec(memory_space=pltpu.VMEM),
        scratch_shapes=[pltpu.VMEM((width, width), jnp.float32)],
        input_output_aliases={} if first == 0 else {0: 0},
        cost_estimate=pl.CostEstimate(flops=n * n * n * 24 * (last - first), bytes_accessed=8 * n * n, transcendentals=0),
        compiler_params=pltpu.CompilerParams(vmem_limit_bytes=32 << 20),
        name="chol",
    )(a)


def place_kernel(idx_ref, me_ref, pts_ref, out_ref):
    rows, width = pts_ref.shape
    nrows = out_ref.shape[0]
    block = idx_ref.shape[1]
    part = block // nrows
    high, mid, tail = split(pts_ref[...])
    base = me_ref[0] * rows
    for h in range(idx_ref.shape[0]):
        idx = jnp.broadcast_to(idx_ref[h : h + 1, :] - base, (8, block)).T[:, :1]
        hot = (idx == lax.broadcasted_iota(jnp.int32, (block, rows), 1)).astype(jnp.float32).astype(jnp.bfloat16)
        total = jnp.dot(hot, tail, preferred_element_type=jnp.float32)
        total += jnp.dot(hot, mid, preferred_element_type=jnp.float32)
        total += jnp.dot(hot, high, preferred_element_type=jnp.float32)
        out_ref[:, h * part : (h + 1) * part, :] = total.reshape(nrows, part, width)


def place(pivots, points):
    nrows = lax.axis_size("rows")
    blocks, block = pivots.shape
    rows, width = points.shape
    vmem = pl.BlockSpec(memory_space=pltpu.VMEM)
    return pl.pallas_call(
        place_kernel,
        out_shape=jax.ShapeDtypeStruct((nrows, blocks * block // nrows, width), jnp.float32),
        in_specs=[vmem, pl.BlockSpec(memory_space=pltpu.SMEM), vmem],
        out_specs=vmem,
        cost_estimate=pl.CostEstimate(flops=12 * block * rows * width, bytes_accessed=8 * rows * width, transcendentals=0),
        compiler_params=pltpu.CompilerParams(vmem_limit_bytes=32 << 20),
        name="place",
    )(pivots, lax.axis_index("rows").reshape(1), points)


def swap(x, mask):
    size = lax.axis_size("cols")
    return lax.ppermute(x, "cols", [(i, i ^ mask) for i in range(size)])


def scatter_sum(x):
    return jnp.sum(lax.all_to_all(x, "rows", 0, 0), axis=0)


def gather_rows(x):
    n = lax.axis_size("rows")
    y = lax.all_to_all(jnp.broadcast_to(x[None], (n,) + x.shape), "rows", 0, 0)
    return y.reshape((n * x.shape[0],) + x.shape[1:])


def tie(*xs):
    return lax.optimization_barrier(xs)


def gauss(left, right):
    cross = lax.dot_general(left, right, (((1,), (1,)), ((), ())), precision=NEAR, preferred_element_type=jnp.float32)
    ln = jnp.sum(left * left, axis=1)
    rn = jnp.sum(right * right, axis=1)
    dist = ln[:, None] + rn[None, :] - 2.0 * cross
    return jnp.exp(-dist / (2.0 * left.shape[1]))


def mul_t(a, b):
    return lax.dot_general(a, b, (((1,), (1,)), ((), ())), precision=HI, preferred_element_type=jnp.float32)


def shards(points, pivots, targets):
    rows_dev = points.shape[0]
    nrows = lax.axis_size("rows")
    ncols = lax.axis_size("cols")
    assert ncols == 4
    block = pivots.shape[1]
    part = block // nrows
    kept = rows_dev // ncols
    col = lax.axis_index("cols")

    goals = targets.T

    def bundle(k):
        at = (col ^ k) * kept
        return [lax.dynamic_slice_in_dim(points, at, kept, 0), lax.dynamic_slice_in_dim(goals, at, kept, 1)]

    placed = place(pivots, points)
    far = swap(jnp.concatenate(bundle(2) + bundle(3), axis=0), 2)
    parts = scatter_sum(placed)
    tall = kept + goals.shape[0]
    rows_a = gather_rows(parts[:part])
    near = swap(jnp.concatenate(bundle(1) + [far[tall:]], axis=0), 1)
    mine = bundle(0)
    own = jnp.concatenate([mine[0], near[:kept], far[:kept], near[tall : tall + kept]], axis=1)
    goal = [mine[1], near[kept:tall], far[kept:tall], near[tall + kept :]]

    two_a = swap(rows_a, 2)
    rows_a, part_b = tie(rows_a, parts[part:])
    rows_b = gather_rows(part_b)
    one_a = swap(rows_a, 1)
    piv_a = jnp.concatenate([rows_a, one_a, two_a, swap(two_a, 1)], axis=1)
    kern_aa = gauss(piv_a, piv_a)
    kern_aa, rows_b = tie(kern_aa, rows_b)
    two_b = swap(rows_b, 2)
    one_b = swap(rows_b, 1)
    state = chol_inverse(kern_aa, 0, 3)
    state, two_b, one_b = tie(state, two_b, one_b)
    piv_b = jnp.concatenate([rows_b, one_b, two_b, swap(two_b, 1)], axis=1)
    pivs = jnp.concatenate([piv_a, piv_b], axis=0)
    kern = gauss(own, pivs)
    pieces = [
        lax.dot_general(g, kern, (((1,), (0,)), ((), ())), precision=HI, preferred_element_type=jnp.float32) for g in goal
    ]
    back = swap(jnp.concatenate([pieces[1], pieces[3]], axis=0), 1)
    deep = goals.shape[0]
    home = pieces[0] + back[:deep]
    away = pieces[2] + back[deep:]
    side = gauss(piv_b, pivs)
    state, away, side = tie(state, away, side)
    returned = swap(away, 2)
    inv_one = chol_inverse(state, 3, 4)
    inv_one, returned = tie(inv_one, returned)
    summed = home + returned
    summed = scatter_sum(summed.reshape(nrows, deep // nrows, summed.shape[1]))
    crossed = mul_t(side[:, :block], inv_one)
    schur = side[:, block:] - mul_t(crossed, crossed)
    schur, summed = tie(schur, summed)
    total = gather_rows(summed)
    inv_two = chol_inverse(schur)
    own_one = mul_t(kern[:, :block], inv_one)
    own_left = kern[:, block:] - mul_t(own_one, crossed)
    inv_two, own_one, own_left, total = tie(inv_two, own_one, own_left, total)
    tot_one = mul_t(total[:, :block], inv_one)
    tot_left = total[:, block:] - mul_t(tot_one, crossed)
    factor = jnp.concatenate([own_one, mul_t(own_left, inv_two)], axis=1)
    final = jnp.concatenate([tot_one, mul_t(tot_left, inv_two)], axis=1)
    projection = final.T * (1.0 / math.sqrt(rows_dev * nrows))
    return (factor, projection)


def solution(mesh):
    return jax.shard_map(
        shards,
        mesh=mesh,
        in_specs=(P("rows", "cols"), P(), P("rows", "cols")),
        out_specs=(P(("rows", "cols"), None), P(None, "cols")),
        check_vma=False,
    )
```

```python
import functools
import math

import jax
import jax.numpy as jnp
from jax import lax
from jax.experimental import pallas as pl
from jax.experimental.pallas import tpu as pltpu
from jax.sharding import PartitionSpec as P


HI = lax.Precision.HIGHEST
NEAR = lax.Precision.HIGH
T = 8
RIDGE = 0.001


def split(x):
    h = x.astype(jnp.bfloat16)
    r = x - h.astype(jnp.float32)
    m = r.astype(jnp.bfloat16)
    return h, m, (r - m.astype(jnp.float32)).astype(jnp.bfloat16)


def left_stack(x):
    h, m, l = split(x)
    return jnp.concatenate([h, h, m, h, m, l], axis=1)


def right_stack(x, axis):
    h, m, l = split(x)
    return jnp.concatenate([h, m, h, l, m, h], axis=axis)


def stack_dot(a, b, axis):
    return lax.dot_general(
        left_stack(a), right_stack(b, axis), (((1,), (axis,)), ((), ())), preferred_element_type=jnp.float32
    )


def diag_inverse(rows, width, sub):
    tiles = width // T
    per = sub // T
    lane = lax.broadcasted_iota(jnp.int32, (T, width), 1)
    sl = lax.broadcasted_iota(jnp.int32, (T, width), 0)
    rows = list(rows)
    scale = [None] * tiles
    for s0 in range(0, tiles, per):
        hi = s0 + per
        recs = []
        for t in range(s0, hi):
            c = {}
            for s in range(t, hi):
                for k in range(T):
                    c[s, k] = jnp.broadcast_to(rows[s][:, T * t + k : T * t + k + 1], (T, width)) + 0.0
            dv = jnp.ones((T, width), jnp.float32)
            for k in range(0, T, 2):
                col = T * t + k

                def row_of(v, i):
                    return jnp.broadcast_to(v[i : i + 1, :], (T, width))

                a = row_of(c[t, k], k)
                b = row_of(c[t, k], k + 1)
                e = row_of(c[t, k + 1], k + 1)
                det = a * e - b * b
                ra = 1.0 / a
                rd = 1.0 / det
                rad = ra * rd
                dv = jnp.where(sl == k, a, jnp.where(sl == k + 1, det * ra, dv))
                r0 = row_of(rows[t], k)
                r1 = row_of(rows[t], k + 1)
                p0 = jnp.where(lane == col, 1.0, r0)
                p1 = jnp.where(lane == col, 0.0, jnp.where(lane == col + 1, 1.0, r1))
                pv = a * p1 - b * jnp.where(lane == col + 1, 0.0, p0)
                new1 = jnp.where(lane == col + 1, 1.0, pv * ra)
                heads = {q: row_of(c[t, q], k) for q in range(k + 2, T)}
                q0 = jnp.where(lane == col + 1, 0.0, p0) * ra
                q1 = pv * rad
                tails, scaled_heads, scaled_tails = {}, {}, {}
                for s in range(t, hi):
                    c0, c1 = c[s, k], c[s, k + 1]
                    if s == t:
                        c0 = jnp.where(sl > k + 1, c0, 0.0)
                        c1 = jnp.where(sl > k + 1, c1, 0.0)
                    w = a * c1 - b * c0
                    for q in range(k + 2, T):
                        if s == t:
                            tails[q] = row_of(w, q)
                            scaled_heads[q] = heads[q] * ra
                            scaled_tails[q] = tails[q] * rad
                            c[s, q] = c[s, q] - c0 * scaled_heads[q] - (w * tails[q]) * rad
                        else:
                            c[s, q] = c[s, q] - c0 * scaled_heads[q] - w * scaled_tails[q]
                    base = rows[s]
                    if s == t:
                        base = jnp.where(((lane == col) | (lane == col + 1)) & (sl > k + 1), 0.0, base)
                        base = jnp.where(sl == k, p0, jnp.where(sl == k + 1, new1, base))
                    else:
                        base = jnp.where((lane == col) | (lane == col + 1), 0.0, base)
                    rows[s] = base - c0 * q0 - w * q1
            scale[t] = lax.rsqrt(dv)
            recs.append(1.0 / dv)
        if hi < tiles:
            x = jnp.concatenate(
                [jnp.where((lane > sl + T * t) & (lane < T * hi), 0.0, rows[t]) for t in range(s0, hi)], axis=0
            )
            w = x * jnp.concatenate(recs, axis=0)
            upd = stack_dot(w[:, T * hi :].T, x, 0)
            for s in range(hi, tiles):
                keep = jnp.where((lane >= T * s0) & (lane < T * hi), 0.0, rows[s])
                rows[s] = keep - upd[T * (s - hi) : T * (s - hi + 1), :]
    out = []
    for t in range(tiles):
        out.append(jnp.where(lane <= sl + T * t, rows[t] * scale[t], 0.0))
    return jnp.concatenate(out, axis=0)


def chol_kernel(width, sub, first, last, a_ref, o_ref, d_ref):
    n = a_ref.shape[0]
    if first == 0:
        o_ref[...] = a_ref[...]
    row = lax.broadcasted_iota(jnp.int32, (n, width), 0)

    def step(j, _):
        off = pl.multiple_of(j * width, width)
        eye = (
            lax.broadcasted_iota(jnp.int32, (width, width), 0) == lax.broadcasted_iota(jnp.int32, (width, width), 1)
        ).astype(jnp.float32)
        d_ref[...] = o_ref[pl.ds(off, width), pl.ds(off, width)] + RIDGE * eye
        m = diag_inverse([d_ref[pl.ds(T * t, T), :] for t in range(width // T)], width, sub)
        col = o_ref[:, pl.ds(off, width)]
        low = jnp.where(row >= off + width, stack_dot(col, m, 1), 0.0)
        o_ref[pl.ds(off, width), pl.ds(off, width)] = eye
        x = stack_dot(m, o_ref[pl.ds(off, width), :], 0)
        o_ref[:, pl.ds(off, width)] = jnp.where(row >= off + width, 0.0, o_ref[:, pl.ds(off, width)])
        o_ref[...] = o_ref[...] - stack_dot(low, x, 0)
        o_ref[pl.ds(off, width), :] = x
        return 0

    lax.fori_loop(first, last, step, 0)
    if last * width == n:
        rr = lax.broadcasted_iota(jnp.int32, (n, n), 0)
        cc = lax.broadcasted_iota(jnp.int32, (n, n), 1)
        o_ref[...] = jnp.where(cc <= rr, o_ref[...], 0.0)


def chol_inverse(a, first=0, last=None, width=128, sub=64):
    n = a.shape[0]
    last = n // width if last is None else last
    return pl.pallas_call(
        functools.partial(chol_kernel, width, sub, first, last),
        out_shape=jax.ShapeDtypeStruct((n, n), jnp.float32),
        in_specs=[pl.BlockSpec(memory_space=pltpu.VMEM)],
        out_specs=pl.BlockSpec(memory_space=pltpu.VMEM),
        scratch_shapes=[pltpu.VMEM((width, width), jnp.float32)],
        input_output_aliases={} if first == 0 else {0: 0},
        cost_estimate=pl.CostEstimate(flops=n * n * n * 24 * (last - first), bytes_accessed=8 * n * n, transcendentals=0),
        compiler_params=pltpu.CompilerParams(vmem_limit_bytes=32 << 20),
        name="chol",
    )(a)


def place_kernel(idx_ref, me_ref, pts_ref, out_ref):
    rows, _ = pts_ref.shape
    nrows = out_ref.shape[1]
    block = idx_ref.shape[1]
    part = block // nrows
    high, mid, tail = split(pts_ref[...])
    base = me_ref[0] * rows
    for h in range(idx_ref.shape[0]):
        idx = jnp.broadcast_to(idx_ref[h : h + 1, :] - base, (8, block)).T[:, :1]
        hot = (idx == lax.broadcasted_iota(jnp.int32, (block, rows), 1)).astype(jnp.float32).astype(jnp.bfloat16)
        total = jnp.dot(hot, tail, preferred_element_type=jnp.float32)
        total += jnp.dot(hot, mid, preferred_element_type=jnp.float32)
        total += jnp.dot(hot, high, preferred_element_type=jnp.float32)
        for r in range(nrows):
            out_ref[h, me_ref[0] ^ r] = total[r * part : (r + 1) * part, :]


def place(pivots, points):
    nrows = lax.axis_size("rows")
    blocks, block = pivots.shape
    rows, width = points.shape
    vmem = pl.BlockSpec(memory_space=pltpu.VMEM)
    return pl.pallas_call(
        place_kernel,
        out_shape=jax.ShapeDtypeStruct((blocks, nrows, block // nrows, width), jnp.float32),
        in_specs=[vmem, pl.BlockSpec(memory_space=pltpu.SMEM), vmem],
        out_specs=vmem,
        cost_estimate=pl.CostEstimate(flops=12 * block * rows * width, bytes_accessed=8 * rows * width, transcendentals=0),
        compiler_params=pltpu.CompilerParams(vmem_limit_bytes=32 << 20),
        name="place",
    )(pivots, lax.axis_index("rows").reshape(1), points)


def swap(x, mask, axis="cols"):
    size = lax.axis_size(axis)
    return lax.ppermute(x, axis, [(i, i ^ mask) for i in range(size)])


def reorder(x):
    n = x.shape[0]
    me = lax.axis_index("rows") % n
    bit = n // 2
    rest = x.shape[1:]
    while bit:
        y = x.reshape((n // (2 * bit), 2, bit) + rest)
        x = jnp.where((me & bit) != 0, y[:, ::-1], y).reshape((n,) + rest)
        bit //= 2
    return x


def scatter_places(x, after=None):
    n = x.shape[0]
    if n > 8:
        return jnp.sum(lax.all_to_all(reorder(x), "rows", 0, 0), axis=0)
    half = x.reshape((n // 2, 2) + x.shape[1:])
    s = half[:, 0] + swap(half[:, 1], 1, "rows")
    moved = [swap(s[k], 2 * k, "rows") for k in range(1, n // 2)]
    if after is not None:
        moved[0] = tie(moved[0], after)[0]
    return sum(moved, s[0])


def gather_places(x, after=None):
    n = lax.axis_size("rows")
    if n > 8:
        return gather_rows(x)
    out = jnp.stack([x] + [swap(x, 2 * k, "rows") for k in range(1, n // 2)])
    out = jnp.stack([out, swap(out, 1, "rows")], axis=1)
    out = out.reshape((n,) + x.shape)
    if after is not None:
        out = tie(out, after)[0]
    return reorder(out).reshape((n * x.shape[0],) + x.shape[1:])


def scatter_sum(x):
    return jnp.sum(lax.all_to_all(x, "rows", 0, 0), axis=0)


def gather_rows(x):
    n = lax.axis_size("rows")
    y = lax.all_to_all(jnp.broadcast_to(x[None], (n,) + x.shape), "rows", 0, 0)
    return y.reshape((n * x.shape[0],) + x.shape[1:])


def tie(*xs):
    return lax.optimization_barrier(xs)


def gauss(left, right):
    cross = lax.dot_general(left, right, (((1,), (1,)), ((), ())), precision=NEAR, preferred_element_type=jnp.float32)
    ln = jnp.sum(left * left, axis=1)
    rn = jnp.sum(right * right, axis=1)
    dist = ln[:, None] + rn[None, :] - 2.0 * cross
    return jnp.exp(-dist / (2.0 * left.shape[1]))


def mul_t(a, b):
    return lax.dot_general(a, b, (((1,), (1,)), ((), ())), precision=HI, preferred_element_type=jnp.float32)


def work(points, pivots, targets):
    rows_dev = points.shape[0]
    nrows = lax.axis_size("rows")
    ncols = lax.axis_size("cols")
    assert ncols == 4
    block = pivots.shape[1]
    kept = rows_dev // ncols
    col = lax.axis_index("cols")

    goals = targets.T

    def bundle(k):
        at = (col ^ k) * kept
        return [lax.dynamic_slice_in_dim(points, at, kept, 0), lax.dynamic_slice_in_dim(goals, at, kept, 1)]

    placed = place(pivots, points)
    far = swap(jnp.concatenate(bundle(2) + bundle(3), axis=0), 2)
    part_a = scatter_places(placed[0])
    tall = kept + goals.shape[0]
    rows_a = gather_places(part_a)
    part_b = scatter_places(placed[1], part_a)
    near = swap(jnp.concatenate(bundle(1) + [far[tall:]], axis=0), 1)
    mine = bundle(0)
    own = jnp.concatenate([mine[0], near[:kept], far[:kept], near[tall : tall + kept]], axis=1)
    goal = [mine[1], near[kept:tall], far[kept:tall], near[tall + kept :]]

    two_a = swap(rows_a, 2)
    one_a = swap(rows_a, 1)
    piv_a = jnp.concatenate([rows_a, one_a, two_a, swap(two_a, 1)], axis=1)
    kern_aa = gauss(piv_a, piv_a)
    rows_b = gather_places(part_b, kern_aa)
    kern_aa, rows_b = tie(kern_aa, rows_b)
    two_b = swap(rows_b, 2)
    one_b = swap(rows_b, 1)
    state = chol_inverse(kern_aa, 0, 3)
    state, two_b, one_b = tie(state, two_b, one_b)
    piv_b = jnp.concatenate([rows_b, one_b, two_b, swap(two_b, 1)], axis=1)
    pivs = jnp.concatenate([piv_a, piv_b], axis=0)
    kern = gauss(own, pivs)
    pieces = lax.dot_general(
        jnp.concatenate(goal, axis=0), kern, (((1,), (0,)), ((), ())), precision=HI, preferred_element_type=jnp.float32
    ).reshape(ncols, goals.shape[0], kern.shape[1])
    back = swap(jnp.concatenate([pieces[1], pieces[3]], axis=0), 1)
    deep = goals.shape[0]
    home = pieces[0] + back[:deep]
    away = pieces[2] + back[deep:]
    side = gauss(tie(piv_b, away)[0], pivs)
    state, away = tie(state, away)
    returned = swap(away, 2)
    inv_one = chol_inverse(state, 3, 4)
    inv_one, returned = tie(inv_one, returned)
    summed = home + returned
    summed = scatter_sum(summed.reshape(nrows, deep // nrows, summed.shape[1]))
    crossed = mul_t(side[:, :block], inv_one)
    schur = side[:, block:] - mul_t(crossed, crossed)
    schur, summed = tie(schur, summed)
    total = gather_rows(summed)
    inv_two = chol_inverse(schur)
    own_one = mul_t(kern[:, :block], inv_one)
    own_left = kern[:, block:] - mul_t(own_one, crossed)
    inv_two, own_one, own_left, total = tie(inv_two, own_one, own_left, total)
    tot_one = mul_t(total[:, :block], inv_one)
    tot_left = total[:, block:] - mul_t(tot_one, crossed)
    factor = jnp.concatenate([own_one, mul_t(own_left, inv_two)], axis=1)
    final = jnp.concatenate([tot_one, mul_t(tot_left, inv_two)], axis=1)
    projection = final.T * (1.0 / math.sqrt(rows_dev * nrows))
    return (factor, projection)


def solution(mesh):
    return jax.shard_map(
        work,
        mesh=mesh,
        in_specs=(P("rows", "cols"), P(), P("rows", "cols")),
        out_specs=(P(("rows", "cols"), None), P(None, "cols")),
        check_vma=False,
    )
```

```python
import functools
import math

import jax
import jax.numpy as jnp
from jax import lax
from jax.experimental import pallas as pl
from jax.experimental.pallas import tpu as pltpu
from jax.sharding import PartitionSpec as P


HI = lax.Precision.HIGHEST
NEAR = lax.Precision.HIGH
T = 8
RIDGE = 0.001


def split(x):
    h = x.astype(jnp.bfloat16)
    r = x - h.astype(jnp.float32)
    m = r.astype(jnp.bfloat16)
    return h, m, (r - m.astype(jnp.float32)).astype(jnp.bfloat16)


def left_stack(x):
    h, m, l = split(x)
    return jnp.concatenate([h, h, m, h, m, l], axis=1)


def right_stack(x, axis):
    h, m, l = split(x)
    return jnp.concatenate([h, m, h, l, m, h], axis=axis)


def stack_dot(a, b, axis):
    return lax.dot_general(
        left_stack(a), right_stack(b, axis), (((1,), (axis,)), ((), ())), preferred_element_type=jnp.float32
    )


def diag_inverse(rows, width, sub):
    tiles = width // T
    per = sub // T
    lane = lax.broadcasted_iota(jnp.int32, (T, width), 1)
    sl = lax.broadcasted_iota(jnp.int32, (T, width), 0)
    rows = list(rows)
    scale = [None] * tiles
    for s0 in range(0, tiles, per):
        hi = s0 + per
        recs = []
        for t in range(s0, hi):
            c = {}
            for s in range(t, hi):
                for k in range(T):
                    c[s, k] = jnp.broadcast_to(rows[s][:, T * t + k : T * t + k + 1], (T, width)) + 0.0
            dv = jnp.ones((T, width), jnp.float32)
            for k in range(0, T, 2):
                col = T * t + k

                def row_of(v, i):
                    return jnp.broadcast_to(v[i : i + 1, :], (T, width))

                a = row_of(c[t, k], k)
                b = row_of(c[t, k], k + 1)
                e = row_of(c[t, k + 1], k + 1)
                det = a * e - b * b
                ra = 1.0 / a
                rd = 1.0 / det
                rad = ra * rd
                dv = jnp.where(sl == k, a, jnp.where(sl == k + 1, det * ra, dv))
                r0 = row_of(rows[t], k)
                r1 = row_of(rows[t], k + 1)
                p0 = jnp.where(lane == col, 1.0, r0)
                p1 = jnp.where(lane == col, 0.0, jnp.where(lane == col + 1, 1.0, r1))
                pv = a * p1 - b * jnp.where(lane == col + 1, 0.0, p0)
                new1 = jnp.where(lane == col + 1, 1.0, pv * ra)
                heads = {q: row_of(c[t, q], k) for q in range(k + 2, T)}
                q0 = jnp.where(lane == col + 1, 0.0, p0) * ra
                q1 = pv * rad
                tails, scaled_heads, scaled_tails = {}, {}, {}
                for s in range(t, hi):
                    c0, c1 = c[s, k], c[s, k + 1]
                    if s == t:
                        c0 = jnp.where(sl > k + 1, c0, 0.0)
                        c1 = jnp.where(sl > k + 1, c1, 0.0)
                    w = a * c1 - b * c0
                    for q in range(k + 2, T):
                        if s == t:
                            tails[q] = row_of(w, q)
                            scaled_heads[q] = heads[q] * ra
                            scaled_tails[q] = tails[q] * rad
                            c[s, q] = c[s, q] - c0 * scaled_heads[q] - (w * tails[q]) * rad
                        else:
                            c[s, q] = c[s, q] - c0 * scaled_heads[q] - w * scaled_tails[q]
                    base = rows[s]
                    if s == t:
                        base = jnp.where(((lane == col) | (lane == col + 1)) & (sl > k + 1), 0.0, base)
                        base = jnp.where(sl == k, p0, jnp.where(sl == k + 1, new1, base))
                    else:
                        base = jnp.where((lane == col) | (lane == col + 1), 0.0, base)
                    rows[s] = base - c0 * q0 - w * q1
            scale[t] = lax.rsqrt(dv)
            recs.append(1.0 / dv)
        if hi < tiles:
            x = jnp.concatenate(
                [jnp.where((lane > sl + T * t) & (lane < T * hi), 0.0, rows[t]) for t in range(s0, hi)], axis=0
            )
            w = x * jnp.concatenate(recs, axis=0)
            h, m, l = split(w)
            left = jnp.concatenate([h, h, m, h, m, l], axis=0)
            upd = lax.dot_general(
                left, right_stack(x, 0), (((0,), (0,)), ((), ())), preferred_element_type=jnp.float32
            )[T * hi :]
            for s in range(hi, tiles):
                keep = jnp.where((lane >= T * s0) & (lane < T * hi), 0.0, rows[s])
                rows[s] = keep - upd[T * (s - hi) : T * (s - hi + 1), :]
    out = []
    for t in range(tiles):
        out.append(jnp.where(lane <= sl + T * t, rows[t] * scale[t], 0.0))
    return jnp.concatenate(out, axis=0)


def chol_steps(width, sub, first, last, o_ref, d_ref):
    n = o_ref.shape[0]
    row = lax.broadcasted_iota(jnp.int32, (n - width, width), 0) + width

    def step(j, _):
        off = pl.multiple_of(j * width, width)
        eye = (
            lax.broadcasted_iota(jnp.int32, (width, width), 0) == lax.broadcasted_iota(jnp.int32, (width, width), 1)
        ).astype(jnp.float32)
        d_ref[...] = o_ref[pl.ds(off, width), pl.ds(off, width)] + RIDGE * eye
        m = diag_inverse([d_ref[pl.ds(T * t, T), :] for t in range(width // T)], width, sub)
        o_ref[pl.ds(off, width), pl.ds(off, width)] = eye
        x = stack_dot(m, o_ref[pl.ds(off, width), :], 0)
        o_ref[pl.ds(off, width), :] = x

        @pl.when(off + width < n)
        def _():
            col = o_ref[width:, pl.ds(off, width)]
            low = jnp.where(row >= off + width, stack_dot(col, m, 1), 0.0)
            o_ref[width:, pl.ds(off, width)] = jnp.where(row >= off + width, 0.0, col)
            o_ref[width:, :] = o_ref[width:, :] - stack_dot(low, x, 0)

        return 0

    lax.fori_loop(first, last, step, 0)
    if last * width == n:
        rr = lax.broadcasted_iota(jnp.int32, (n, n), 0)
        cc = lax.broadcasted_iota(jnp.int32, (n, n), 1)
        o_ref[...] = jnp.where(cc <= rr, o_ref[...], 0.0)


def chol_kernel(width, sub, first, last, a_ref, o_ref, d_ref):
    del a_ref
    chol_steps(width, sub, first, last, o_ref, d_ref)


VMEM = pl.BlockSpec(memory_space=pltpu.VMEM)


def chol_inverse(a, first, last, width=128, sub=64):
    n = a.shape[0]
    return pl.pallas_call(
        functools.partial(chol_kernel, width, sub, first, last),
        out_shape=jax.ShapeDtypeStruct((n, n), jnp.float32),
        in_specs=[VMEM],
        out_specs=VMEM,
        scratch_shapes=[pltpu.VMEM((width, width), jnp.float32)],
        input_output_aliases={0: 0},
        cost_estimate=pl.CostEstimate(flops=n * n * n * 24 * (last - first), bytes_accessed=8 * n * n, transcendentals=0),
        compiler_params=pltpu.CompilerParams(vmem_limit_bytes=12 << 20),
        name="chol",
    )(a)


def schur_kernel(side_ref, one_ref, cross_ref, schur_ref):
    n = one_ref.shape[0]
    crossed = stack_dot(side_ref[:, :n], one_ref[...], 1)
    cross_ref[...] = crossed
    schur_ref[...] = side_ref[:, n:] - stack_dot(crossed, crossed, 1)


def schur_of(side, one):
    n = one.shape[0]
    shape = jax.ShapeDtypeStruct((n, n), jnp.float32)
    return pl.pallas_call(
        schur_kernel,
        out_shape=(shape, shape),
        in_specs=[VMEM] * 2,
        out_specs=(VMEM, VMEM),
        cost_estimate=pl.CostEstimate(flops=24 * n * n * n, bytes_accessed=20 * n * n, transcendentals=0),
        compiler_params=pltpu.CompilerParams(vmem_limit_bytes=24 << 20),
        name="schur",
    )(side, one)


def finish_kernel(
    width, sub, first, scale, a_ref, k1_ref, k2_ref, tot_ref, one_ref, cross_ref, factor_ref, proj_ref, two_ref, d_ref, w_ref
):
    n = one_ref.shape[0]
    rows = k1_ref.shape[0]
    del a_ref
    chol_steps(width, sub, first, n // width, two_ref, d_ref)
    w_ref[:rows, :n] = k1_ref[...]
    w_ref[:rows, n:] = k2_ref[...]
    w_ref[rows:, :] = tot_ref[...]
    one = stack_dot(w_ref[:, :n], one_ref[...], 1)
    factor_ref[:, :n] = one[:rows]
    proj_ref[:, :n] = one[rows:] * scale
    left = w_ref[:, n:] - stack_dot(one, cross_ref[...], 1)
    two = stack_dot(left, two_ref[...], 1)
    factor_ref[:, n:] = two[:rows]
    proj_ref[:, n:] = two[rows:] * scale


def finish(scale, state, kern_a, kern_b, tot, one, crossed, first, width=128, sub=64):
    rows = kern_a.shape[0]
    deep, both = tot.shape
    return pl.pallas_call(
        functools.partial(finish_kernel, width, sub, first, scale),
        out_shape=(
            jax.ShapeDtypeStruct((rows, both), jnp.float32),
            jax.ShapeDtypeStruct((deep, both), jnp.float32),
            jax.ShapeDtypeStruct(state.shape, jnp.float32),
        ),
        in_specs=[VMEM] * 6,
        out_specs=(VMEM, VMEM, VMEM),
        input_output_aliases={0: 2},
        scratch_shapes=[
            pltpu.VMEM((width, width), jnp.float32),
            pltpu.VMEM((rows + deep, both), jnp.float32),
        ],
        cost_estimate=pl.CostEstimate(flops=9 * (rows + deep) * both * both // 2, bytes_accessed=16 * rows * both, transcendentals=0),
        compiler_params=pltpu.CompilerParams(vmem_limit_bytes=24 << 20),
        name="finish",
    )(state, kern_a, kern_b, tot, one, crossed)[:2]


def place_kernel(idx_ref, me_ref, pts_ref, out_ref):
    rows, _ = pts_ref.shape
    nrows = out_ref.shape[1]
    block = idx_ref.shape[1]
    part = block // nrows
    high, mid, tail = split(pts_ref[...])
    base = me_ref[0] * rows
    for h in range(idx_ref.shape[0]):
        idx = jnp.broadcast_to(idx_ref[h : h + 1, :] - base, (8, block)).T[:, :1]
        hot = (idx == lax.broadcasted_iota(jnp.int32, (block, rows), 1)).astype(jnp.float32).astype(jnp.bfloat16)
        total = jnp.dot(hot, tail, preferred_element_type=jnp.float32)
        total += jnp.dot(hot, mid, preferred_element_type=jnp.float32)
        total += jnp.dot(hot, high, preferred_element_type=jnp.float32)
        for r in range(nrows):
            out_ref[h, me_ref[0] ^ r] = total[r * part : (r + 1) * part, :]


def place(pivots, points):
    nrows = lax.axis_size("rows")
    blocks, block = pivots.shape
    rows, width = points.shape
    vmem = pl.BlockSpec(memory_space=pltpu.VMEM)
    return pl.pallas_call(
        place_kernel,
        out_shape=jax.ShapeDtypeStruct((blocks, nrows, block // nrows, width), jnp.float32),
        in_specs=[vmem, pl.BlockSpec(memory_space=pltpu.SMEM), vmem],
        out_specs=vmem,
        cost_estimate=pl.CostEstimate(flops=12 * block * rows * width, bytes_accessed=8 * rows * width, transcendentals=0),
        compiler_params=pltpu.CompilerParams(vmem_limit_bytes=32 << 20),
        name="place",
    )(pivots, lax.axis_index("rows").reshape(1), points)


def swap(x, mask, axis="cols"):
    size = lax.axis_size(axis)
    return lax.ppermute(x, axis, [(i, i ^ mask) for i in range(size)])


def reorder(x, me):
    n = x.shape[0]
    bit = n // 2
    rest = x.shape[1:]
    while bit:
        y = x.reshape((n // (2 * bit), 2, bit) + rest)
        x = jnp.where((me & bit) != 0, y[:, ::-1], y).reshape((n,) + rest)
        bit //= 2
    return x


def scatter_places(x, after=None):
    n = x.shape[0]
    if n > 8:
        return jnp.sum(lax.all_to_all(reorder(x, lax.axis_index("rows")), "rows", 0, 0), axis=0)
    half = x.reshape((n // 2, 2) + x.shape[1:])
    s = half[:, 0] + swap(half[:, 1], 1, "rows")
    moved = [swap(s[k], 2 * k, "rows") for k in range(1, n // 2)]
    if after is not None:
        moved[0] = tie(moved[0], after)[0]
    return sum(moved, s[0])


def gather_places(x, after=None):
    n = lax.axis_size("rows")
    if n > 8:
        return gather_rows(x)
    out = jnp.stack([x] + [swap(x, 2 * k, "rows") for k in range(1, n // 2)])
    out = jnp.stack([out, swap(out, 1, "rows")], axis=1)
    out = out.reshape((n,) + x.shape)
    if after is not None:
        out = tie(out, after)[0]
    return reorder(out, lax.axis_index("rows")).reshape((n * x.shape[0],) + x.shape[1:])


def scatter_sum(x):
    return jnp.sum(lax.all_to_all(x, "rows", 0, 0), axis=0)


def gather_rows(x):
    n = lax.axis_size("rows")
    y = lax.all_to_all(jnp.broadcast_to(x[None], (n,) + x.shape), "rows", 0, 0)
    return y.reshape((n * x.shape[0],) + x.shape[1:])


def sum_rows(x, schur):
    n = lax.axis_size("rows")
    if n > 8:
        total = gather_rows(scatter_sum(x.reshape((n, x.shape[0] // n) + x.shape[1:])))
        return total, chol_inverse(schur, 0, 1)
    part = lax.axis_index("rows") // 2
    half = n // 2
    deep = x.shape[0] // half
    x, schur = tie(x + swap(x, 1, "rows"), schur)
    cuts = [lax.dynamic_slice_in_dim(x, (part ^ k) * deep, deep, 0) for k in range(half)]
    moved = [swap(cuts[k], 2 * k, "rows") for k in range(1, half)]
    state = chol_inverse(schur, 0, 1)
    state, moved[0] = tie(state, moved[0])
    one = sum(moved, cuts[0])
    out = jnp.stack([one] + [swap(one, 2 * k, "rows") for k in range(1, half)])
    return reorder(out, part).reshape(x.shape), state


def tie(*xs):
    return lax.optimization_barrier(xs)


def norms(x):
    return jnp.sum(x * x, axis=1)


def gauss(left, right, ln, rn):
    cross = lax.dot_general(left, right, (((1,), (1,)), ((), ())), precision=NEAR, preferred_element_type=jnp.float32)
    dist = ln[:, None] + rn[None, :] - 2.0 * cross
    return jnp.exp(-dist / (2.0 * left.shape[1]))


CUT = 3


def work(points, pivots, targets):
    rows_dev = points.shape[0]
    nrows = lax.axis_size("rows")
    ncols = lax.axis_size("cols")
    assert ncols == 4
    block = pivots.shape[1]
    kept = rows_dev // ncols
    col = lax.axis_index("cols")

    goals = targets.T

    def bundle(k):
        at = (col ^ k) * kept
        return [lax.dynamic_slice_in_dim(points, at, kept, 0), lax.dynamic_slice_in_dim(goals, at, kept, 1)]

    placed = place(pivots, points)
    far = swap(jnp.concatenate(bundle(2) + bundle(3), axis=0), 2)
    part_a = scatter_places(placed[0])
    tall = kept + goals.shape[0]
    rows_a = gather_places(part_a)
    part_b = scatter_places(placed[1], part_a)
    near = swap(jnp.concatenate(bundle(1) + [far[tall:]], axis=0), 1)
    mine = bundle(0)
    own = jnp.concatenate([mine[0], near[:kept], far[:kept], near[tall : tall + kept]], axis=1)
    goal = [mine[1], near[kept:tall], far[kept:tall], near[tall + kept :]]

    two_a = swap(rows_a, 2)
    one_a = swap(rows_a, 1)
    piv_a = jnp.concatenate([rows_a, one_a, two_a, swap(two_a, 1)], axis=1)
    norms_a = norms(piv_a)
    kern_aa = gauss(piv_a, piv_a, norms_a, norms_a)
    rows_b = gather_places(part_b, kern_aa)
    kern_aa, rows_b = tie(kern_aa, rows_b)
    two_b = swap(rows_b, 2)
    one_b = swap(rows_b, 1)
    goal = jnp.concatenate(goal, axis=0)
    deep = goals.shape[0]

    own_norms = norms(own)

    def against(pivs, their):
        kern = gauss(own, pivs, own_norms, their)
        return kern, lax.dot_general(
            goal, kern, (((1,), (0,)), ((), ())), precision=HI, preferred_element_type=jnp.float32
        ).reshape(ncols, deep, block)

    state = chol_inverse(kern_aa, 0, CUT)
    state, piv_a = tie(state, piv_a)
    kern_a, sums_a = against(piv_a, norms_a)
    state, two_b, one_b, sums_a = tie(state, two_b, one_b, sums_a)
    piv_b = jnp.concatenate([rows_b, one_b, two_b, swap(two_b, 1)], axis=1)
    norms_b = norms(piv_b)
    kern_b, sums_b = against(piv_b, norms_b)

    def both(k):
        return jnp.concatenate([sums_a[k], sums_b[k]], axis=1)

    back = swap(jnp.concatenate([both(1), both(3)], axis=0), 1)
    away = both(2) + back[deep:]
    state, away = tie(state, away)
    home = both(0) + back[:deep]
    returned = swap(away, 2)
    inv_one = chol_inverse(state, CUT, 4)
    side = gauss(
        tie(piv_b, inv_one)[0], jnp.concatenate([piv_a, piv_b], axis=0), norms_b, jnp.concatenate([norms_a, norms_b])
    )
    side, returned = tie(side, returned)
    summed = home + returned
    side, _ = tie(side, summed)
    crossed, schur = schur_of(side, inv_one)
    total, state = sum_rows(summed, schur)
    state = chol_inverse(state, 1, 3)
    factor, projection = finish(
        1.0 / math.sqrt(rows_dev * nrows), state, kern_a, kern_b, total, inv_one, crossed, 3
    )
    return (factor, projection.T)


def solution(mesh):
    return jax.shard_map(
        work,
        mesh=mesh,
        in_specs=(P("rows", "cols"), P(), P("rows", "cols")),
        out_specs=(P(("rows", "cols"), None), P(None, "cols")),
        check_vma=False,
    )
```

```python
import functools
import math

import jax
import jax.numpy as jnp
from jax import lax
from jax.experimental import pallas as pl
from jax.experimental.pallas import tpu as pltpu
from jax.sharding import PartitionSpec as P


HI = lax.Precision.HIGHEST
NEAR = lax.Precision.HIGH
T = 8
RIDGE = 0.001


def split(x):
    h = x.astype(jnp.bfloat16)
    r = x - h.astype(jnp.float32)
    m = r.astype(jnp.bfloat16)
    return h, m, (r - m.astype(jnp.float32)).astype(jnp.bfloat16)


def left_stack(x):
    h, m, l = split(x)
    return jnp.concatenate([h, h, m, h, m, l], axis=1)


def right_stack(x, axis):
    h, m, l = split(x)
    return jnp.concatenate([h, m, h, l, m, h], axis=axis)


def stack_dot(a, b, axis):
    return lax.dot_general(
        left_stack(a), right_stack(b, axis), (((1,), (axis,)), ((), ())), preferred_element_type=jnp.float32
    )


def stacked(a, weights):
    return lax.dot_general(left_stack(a), weights, (((1,), (1,)), ((), ())), preferred_element_type=jnp.float32)


def diag_inverse(rows, width, sub):
    tiles = width // T
    per = sub // T
    lane = lax.broadcasted_iota(jnp.int32, (T, width), 1)
    sl = lax.broadcasted_iota(jnp.int32, (T, width), 0)
    rows = list(rows)
    scale = [None] * tiles
    for s0 in range(0, tiles, per):
        hi = s0 + per
        recs = []
        for t in range(s0, hi):
            c = {}
            for s in range(t, hi):
                for k in range(T):
                    c[s, k] = jnp.broadcast_to(rows[s][:, T * t + k : T * t + k + 1], (T, width)) + 0.0
            dv = jnp.ones((T, width), jnp.float32)
            for k in range(0, T, 2):
                col = T * t + k

                def row_of(v, i):
                    return jnp.broadcast_to(v[i : i + 1, :], (T, width))

                a = row_of(c[t, k], k)
                b = row_of(c[t, k], k + 1)
                e = row_of(c[t, k + 1], k + 1)
                det = a * e - b * b
                ra = 1.0 / a
                rd = 1.0 / det
                rad = ra * rd
                dv = jnp.where(sl == k, a, jnp.where(sl == k + 1, det * ra, dv))
                r0 = row_of(rows[t], k)
                r1 = row_of(rows[t], k + 1)
                p0 = jnp.where(lane == col, 1.0, r0)
                p1 = jnp.where(lane == col, 0.0, jnp.where(lane == col + 1, 1.0, r1))
                pv = a * p1 - b * jnp.where(lane == col + 1, 0.0, p0)
                new1 = jnp.where(lane == col + 1, 1.0, pv * ra)
                heads = {q: row_of(c[t, q], k) for q in range(k + 2, T)}
                q0 = jnp.where(lane == col + 1, 0.0, p0) * ra
                q1 = pv * rad
                tails, scaled_heads, scaled_tails = {}, {}, {}
                for s in range(t, hi):
                    c0, c1 = c[s, k], c[s, k + 1]
                    if s == t:
                        c0 = jnp.where(sl > k + 1, c0, 0.0)
                        c1 = jnp.where(sl > k + 1, c1, 0.0)
                    w = a * c1 - b * c0
                    for q in range(k + 2, T):
                        if s == t:
                            tails[q] = row_of(w, q)
                            scaled_heads[q] = heads[q] * ra
                            scaled_tails[q] = tails[q] * rad
                            c[s, q] = c[s, q] - c0 * scaled_heads[q] - (w * tails[q]) * rad
                        else:
                            c[s, q] = c[s, q] - c0 * scaled_heads[q] - w * scaled_tails[q]
                    base = rows[s]
                    if s == t:
                        base = jnp.where(((lane == col) | (lane == col + 1)) & (sl > k + 1), 0.0, base)
                        base = jnp.where(sl == k, p0, jnp.where(sl == k + 1, new1, base))
                    else:
                        base = jnp.where((lane == col) | (lane == col + 1), 0.0, base)
                    rows[s] = base - c0 * q0 - w * q1
            scale[t] = lax.rsqrt(dv)
            recs.append(1.0 / dv)
        if hi < tiles:
            x = jnp.concatenate(
                [jnp.where((lane > sl + T * t) & (lane < T * hi), 0.0, rows[t]) for t in range(s0, hi)], axis=0
            )
            w = x * jnp.concatenate(recs, axis=0)
            h, m, l = split(w)
            left = jnp.concatenate([h, h, m, h, m, l], axis=0)
            upd = lax.dot_general(
                left, right_stack(x, 0), (((0,), (0,)), ((), ())), preferred_element_type=jnp.float32
            )[T * hi :]
            for s in range(hi, tiles):
                keep = jnp.where((lane >= T * s0) & (lane < T * hi), 0.0, rows[s])
                rows[s] = keep - upd[T * (s - hi) : T * (s - hi + 1), :]
    out = []
    for t in range(tiles):
        out.append(jnp.where(lane <= sl + T * t, rows[t] * scale[t], 0.0))
    return jnp.concatenate(out, axis=0)


def chol_steps(width, sub, first, last, o_ref, d_ref):
    n = o_ref.shape[0]
    row = lax.broadcasted_iota(jnp.int32, (n - width, width), 0) + width

    def step(j, _):
        off = pl.multiple_of(j * width, width)
        eye = (
            lax.broadcasted_iota(jnp.int32, (width, width), 0) == lax.broadcasted_iota(jnp.int32, (width, width), 1)
        ).astype(jnp.float32)
        d_ref[...] = o_ref[pl.ds(off, width), pl.ds(off, width)] + RIDGE * eye
        m = diag_inverse([d_ref[pl.ds(T * t, T), :] for t in range(width // T)], width, sub)
        o_ref[pl.ds(off, width), pl.ds(off, width)] = eye
        x = stack_dot(m, o_ref[pl.ds(off, width), :], 0)
        o_ref[pl.ds(off, width), :] = x

        @pl.when(off + width < n)
        def _():
            col = o_ref[width:, pl.ds(off, width)]
            low = jnp.where(row >= off + width, stack_dot(col, m, 1), 0.0)
            o_ref[width:, pl.ds(off, width)] = jnp.where(row >= off + width, 0.0, col)
            o_ref[width:, :] = o_ref[width:, :] - stack_dot(low, x, 0)

        return 0

    lax.fori_loop(first, last, step, 0)
    if last * width == n:
        rr = lax.broadcasted_iota(jnp.int32, (n, n), 0)
        cc = lax.broadcasted_iota(jnp.int32, (n, n), 1)
        o_ref[...] = jnp.where(cc <= rr, o_ref[...], 0.0)


def chol_kernel(width, sub, first, last, a_ref, o_ref, d_ref):
    del a_ref
    chol_steps(width, sub, first, last, o_ref, d_ref)


VMEM = pl.BlockSpec(memory_space=pltpu.VMEM)


def chol_inverse(a, first, last, width=128, sub=64):
    n = a.shape[0]
    return pl.pallas_call(
        functools.partial(chol_kernel, width, sub, first, last),
        out_shape=jax.ShapeDtypeStruct((n, n), jnp.float32),
        in_specs=[VMEM],
        out_specs=VMEM,
        scratch_shapes=[pltpu.VMEM((width, width), jnp.float32)],
        input_output_aliases={0: 0},
        cost_estimate=pl.CostEstimate(flops=n * n * n * 24 * (last - first), bytes_accessed=8 * n * n, transcendentals=0),
        compiler_params=pltpu.CompilerParams(vmem_limit_bytes=12 << 20),
        name="chol",
    )(a)


def schur_kernel(side_ref, one_ref, k1_ref, k2_ref, cross_ref, schur_ref, own_ref):
    n = one_ref.shape[0]
    weights = right_stack(one_ref[...], 1)
    crossed = stacked(side_ref[:, :n], weights)
    cross_ref[...] = crossed
    weights_too = right_stack(crossed, 1)
    schur_ref[...] = side_ref[:, n:] - stacked(crossed, weights_too)
    first = stacked(k1_ref[...], weights)
    own_ref[:, :n] = first
    own_ref[:, n:] = k2_ref[...] - stacked(first, weights_too)


def schur_of(side, one, k1, k2):
    n = one.shape[0]
    shape = jax.ShapeDtypeStruct((n, n), jnp.float32)
    own = jax.ShapeDtypeStruct((k1.shape[0], 2 * n), jnp.float32)
    return pl.pallas_call(
        schur_kernel,
        out_shape=(shape, shape, own),
        in_specs=[VMEM] * 4,
        out_specs=(VMEM, VMEM, VMEM),
        cost_estimate=pl.CostEstimate(flops=36 * n * n * n, bytes_accessed=30 * n * n, transcendentals=0),
        compiler_params=pltpu.CompilerParams(vmem_limit_bytes=28 << 20),
        name="schur",
    )(side, one, k1, k2)


def finish_kernel(
    width, sub, first, scale, a_ref, own_ref, tot_ref, one_ref, cross_ref, factor_ref, proj_ref, two_ref, d_ref, w_ref
):
    n = one_ref.shape[0]
    rows = own_ref.shape[0]
    del a_ref
    chol_steps(width, sub, first, n // width, two_ref, d_ref)
    one = stack_dot(tot_ref[:, :n], one_ref[...], 1)
    proj_ref[:, :n] = one * scale
    w_ref[rows:, :] = tot_ref[:, n:] - stack_dot(one, cross_ref[...], 1)
    w_ref[:rows, :] = own_ref[:, n:]
    two = stack_dot(w_ref[...], two_ref[...], 1)
    factor_ref[:, :n] = own_ref[:, :n]
    factor_ref[:, n:] = two[:rows]
    proj_ref[:, n:] = two[rows:] * scale


def finish(scale, state, own, tot, one, crossed, first, width=128, sub=64):
    rows = own.shape[0]
    deep, both = tot.shape
    return pl.pallas_call(
        functools.partial(finish_kernel, width, sub, first, scale),
        out_shape=(
            jax.ShapeDtypeStruct((rows, both), jnp.float32),
            jax.ShapeDtypeStruct((deep, both), jnp.float32),
            jax.ShapeDtypeStruct(state.shape, jnp.float32),
        ),
        in_specs=[VMEM] * 5,
        out_specs=(VMEM, VMEM, VMEM),
        input_output_aliases={0: 2},
        scratch_shapes=[
            pltpu.VMEM((width, width), jnp.float32),
            pltpu.VMEM((rows + deep, both // 2), jnp.float32),
        ],
        cost_estimate=pl.CostEstimate(flops=9 * (rows + deep) * both * both // 2, bytes_accessed=16 * rows * both, transcendentals=0),
        compiler_params=pltpu.CompilerParams(vmem_limit_bytes=24 << 20),
        name="finish",
    )(state, own, tot, one, crossed)[:2]


def place_kernel(which, idx_ref, me_ref, pts_ref, keep_ref, send_ref):
    rows, _ = pts_ref.shape
    half, part, _ = keep_ref.shape
    block = idx_ref.shape[1]
    me = me_ref[0]
    idx = jnp.broadcast_to(idx_ref[which : which + 1, :] - me * rows, (8, block)).T[:, :1]
    hot = (idx == lax.broadcasted_iota(jnp.int32, (block, rows), 1)).astype(jnp.float32).astype(jnp.bfloat16)
    high, mid, tail = split(pts_ref[...])
    total = jnp.dot(hot, tail, preferred_element_type=jnp.float32)
    total += jnp.dot(hot, mid, preferred_element_type=jnp.float32)
    total += jnp.dot(hot, high, preferred_element_type=jnp.float32)

    def put(even_ref, odd_ref):
        for r in range(2 * half):
            ref = even_ref if r % 2 == 0 else odd_ref
            ref[(me ^ r) // 2] = total[r * part : (r + 1) * part, :]

    pl.when(me % 2 == 0)(lambda: put(keep_ref, send_ref))
    pl.when(me % 2 == 1)(lambda: put(send_ref, keep_ref))


def place(pivots, points, which):
    nrows = lax.axis_size("rows")
    block = pivots.shape[1]
    rows, width = points.shape
    shape = jax.ShapeDtypeStruct((nrows // 2, block // nrows, width), jnp.float32)
    return pl.pallas_call(
        functools.partial(place_kernel, which),
        out_shape=(shape, shape),
        in_specs=[VMEM, pl.BlockSpec(memory_space=pltpu.SMEM), VMEM],
        out_specs=(VMEM, VMEM),
        cost_estimate=pl.CostEstimate(flops=6 * block * rows * width, bytes_accessed=8 * rows * width, transcendentals=0),
        compiler_params=pltpu.CompilerParams(vmem_limit_bytes=32 << 20),
        name="place",
    )(pivots, lax.axis_index("rows").reshape(1), points)


def swap(x, mask, axis="cols"):
    size = lax.axis_size(axis)
    return lax.ppermute(x, axis, [(i, i ^ mask) for i in range(size)])


def reorder(x, me):
    n = x.shape[0]
    bit = n // 2
    rest = x.shape[1:]
    while bit:
        y = x.reshape((n // (2 * bit), 2, bit) + rest)
        x = jnp.where((me & bit) != 0, y[:, ::-1], y).reshape((n,) + rest)
        bit //= 2
    return x


def scatter_places(x, after=None):
    keep, send = x
    n = 2 * keep.shape[0]
    if n > 8:
        x = jnp.stack([keep, send], axis=1).reshape((n,) + keep.shape[1:])
        return jnp.sum(lax.all_to_all(reorder(x, lax.axis_index("rows")), "rows", 0, 0), axis=0)
    s = keep + swap(send, 1, "rows")
    moved = [swap(s[k], 2 * k, "rows") for k in range(1, n // 2)]
    if after is not None:
        moved[0] = tie(moved[0], after)[0]
    return sum(moved, s[0])


def gather_places(x, after=None):
    n = lax.axis_size("rows")
    if n > 8:
        return gather_rows(x)
    out = jnp.stack([x] + [swap(x, 2 * k, "rows") for k in range(1, n // 2)])
    out = jnp.stack([out, swap(out, 1, "rows")], axis=1)
    out = out.reshape((n,) + x.shape)
    if after is not None:
        out = tie(out, after)[0]
    return reorder(out, lax.axis_index("rows")).reshape((n * x.shape[0],) + x.shape[1:])


def scatter_sum(x):
    return jnp.sum(lax.all_to_all(x, "rows", 0, 0), axis=0)


def gather_rows(x):
    n = lax.axis_size("rows")
    y = lax.all_to_all(jnp.broadcast_to(x[None], (n,) + x.shape), "rows", 0, 0)
    return y.reshape((n * x.shape[0],) + x.shape[1:])


def sum_rows(x, schur):
    n = lax.axis_size("rows")
    if n > 8:
        total = gather_rows(scatter_sum(x.reshape((n, x.shape[0] // n) + x.shape[1:])))
        return total, chol_inverse(schur, 0, 1)
    part = lax.axis_index("rows") // 2
    half = n // 2
    deep = x.shape[0] // half
    x, schur = tie(x + swap(x, 1, "rows"), schur)
    cuts = [lax.dynamic_slice_in_dim(x, (part ^ k) * deep, deep, 0) for k in range(half)]
    moved = [swap(cuts[k], 2 * k, "rows") for k in range(1, half)]
    state = chol_inverse(schur, 0, 1)
    state, moved[0] = tie(state, moved[0])
    one = sum(moved, cuts[0])
    out = jnp.stack([one] + [swap(one, 2 * k, "rows") for k in range(1, half)])
    return reorder(out, part).reshape(x.shape), state


def tie(*xs):
    return lax.optimization_barrier(xs)


def norms(x):
    return jnp.sum(x * x, axis=1)


def gauss(left, right, ln, rn):
    cross = lax.dot_general(left, right, (((1,), (1,)), ((), ())), precision=NEAR, preferred_element_type=jnp.float32)
    dist = ln[:, None] + rn[None, :] - 2.0 * cross
    return jnp.exp(-dist / (2.0 * left.shape[1]))


CUT = 2


def work(points, pivots, targets):
    rows_dev = points.shape[0]
    nrows = lax.axis_size("rows")
    ncols = lax.axis_size("cols")
    assert ncols == 4
    block = pivots.shape[1]
    kept = rows_dev // ncols
    col = lax.axis_index("cols")

    goals = targets.T

    def bundle(k):
        at = (col ^ k) * kept
        return [lax.dynamic_slice_in_dim(points, at, kept, 0), lax.dynamic_slice_in_dim(goals, at, kept, 1)]

    placed = [place(pivots, points, h) for h in range(2)]
    far = swap(jnp.concatenate(bundle(2) + bundle(3), axis=0), 2)
    part_a = scatter_places(placed[0])
    tall = kept + goals.shape[0]
    rows_a = gather_places(part_a)
    part_b = scatter_places(placed[1], part_a)
    near = swap(jnp.concatenate(bundle(1) + [far[tall:]], axis=0), 1)
    mine = bundle(0)
    own = jnp.concatenate([mine[0], near[:kept], far[:kept], near[tall : tall + kept]], axis=1)
    goal = [mine[1], near[kept:tall], far[kept:tall], near[tall + kept :]]

    two_a = swap(rows_a, 2)
    one_a = swap(rows_a, 1)
    piv_a = jnp.concatenate([rows_a, one_a, two_a, swap(two_a, 1)], axis=1)
    norms_a = norms(piv_a)
    kern_aa = gauss(piv_a, piv_a, norms_a, norms_a)
    rows_b = gather_places(part_b, rows_a)
    two_b = swap(rows_b, 2)
    one_b = swap(rows_b, 1)
    goal = jnp.concatenate(goal, axis=0)
    deep = goals.shape[0]

    own_norms = norms(own)

    def against(pivs, their):
        kern = gauss(own, pivs, own_norms, their)
        return kern, lax.dot_general(
            goal, kern, (((1,), (0,)), ((), ())), precision=HI, preferred_element_type=jnp.float32
        ).reshape(ncols, deep, block)

    state = chol_inverse(kern_aa, 0, CUT)
    state, piv_a = tie(state, piv_a)
    kern_a, sums_a = against(piv_a, norms_a)
    state, two_b, one_b, sums_a = tie(state, two_b, one_b, sums_a)
    piv_b = jnp.concatenate([rows_b, one_b, two_b, swap(two_b, 1)], axis=1)
    norms_b = norms(piv_b)
    kern_b, sums_b = against(piv_b, norms_b)

    def both(k):
        return jnp.concatenate([sums_a[k], sums_b[k]], axis=1)

    back = swap(jnp.concatenate([both(1), both(3)], axis=0), 1)
    away = both(2) + back[deep:]
    state, away = tie(state, away)
    home = both(0) + back[:deep]
    returned = swap(away, 2)
    inv_one = chol_inverse(state, CUT, 4)
    side = gauss(
        tie(piv_b, inv_one)[0], jnp.concatenate([piv_a, piv_b], axis=0), norms_b, jnp.concatenate([norms_a, norms_b])
    )
    side, returned = tie(side, returned)
    summed = home + returned
    side, _ = tie(side, summed)
    crossed, schur, factors = schur_of(side, inv_one, kern_a, kern_b)
    total, state = sum_rows(summed, schur)
    state = chol_inverse(state, 1, 3)
    factor, projection = finish(
        1.0 / math.sqrt(rows_dev * nrows), state, factors, total, inv_one, crossed, 3
    )
    return (factor, projection.T)


def solution(mesh):
    return jax.shard_map(
        work,
        mesh=mesh,
        in_specs=(P("rows", "cols"), P(), P("rows", "cols")),
        out_specs=(P(("rows", "cols"), None), P(None, "cols")),
        check_vma=False,
    )
```
